512 devices in a mesh: row: 32 (over y, z_hi, core), col: 16 (over z_lo, x).
Axes of the slice: x: 4, y: 4, z: 16 (z_hi: 4, z_lo: 4; z = z_hi * 4 + z_lo), core: 2. Of those that a mesh axis runs over, the one named last changes fastest.
Arguments:
- trailing: bfloat16 [16384, 32768], P('row', 'col'), may hold values from -6 to 6
- col_u: bfloat16 [32, 512, 64], P('row', 'col'), may hold values from -6 to 6
- col_v: bfloat16 [32, 512, 64], P('row', 'col'), may hold values from -0.75 to 0.75
- row_u: bfloat16 [64, 512, 64], P('col', 'row'), may hold values from -6 to 6
- row_v: bfloat16 [64, 512, 64], P('col', 'row'), may hold values from -0.03125 to 0.03125
- diag_lower_inv: float32 [512, 512], replicated, may hold values from -0.176776695 to 1, as said below
- diag_upper_inv: float32 [512, 512], replicated, may hold values from -0.176776695 to 2, as said below
Outputs:
- schur: bfloat16 [16384, 32768], P('row', 'col')
The draws below stay inside these ranges and needn't reach their ends.
Inputs may be any that keep to these rules, and one draw needn't show every extreme that they name: `diag_lower_inv`: lower triangular with unit diagonal. `diag_upper_inv`: upper triangular with diagonal entries between 0.5 and 2.
All inputs are finite; a program needn't handle non-finite values.
Results may differ from the reference program's by a relative error of at most 0.0054.
Values may be sent and summed in bfloat16 or wider, within the bound.
No kernel may reach another device: no remote copies, remote signals or barrier semaphores. Data moves between devices by JAX's collectives and lax.ppermute only.
A program may use at most 64 MiB of HBM per device.

```python
import jax
import jax.numpy as jnp
from jax import lax

B = 512
R = 64
MT = 32
NT = 64


def draw_diag_lower_inv(key, part):
    noise = jnp.clip(jax.random.normal(jax.random.fold_in(key, 11), (B, B), jnp.float32), -4.0, 4.0)
    below = jnp.tril(noise, -1) / jnp.sqrt(jnp.float32(B))
    return below + jnp.eye(B, dtype=jnp.float32)


def draw_diag_upper_inv(key, part):
    noise = jnp.clip(jax.random.normal(jax.random.fold_in(key, 23), (B, B), jnp.float32), -4.0, 4.0)
    above = jnp.triu(noise, 1) / jnp.sqrt(jnp.float32(B))
    pivots = jax.random.uniform(jax.random.fold_in(key, 37), (B,), jnp.float32, 0.5, 2.0)
    return above + jnp.diag(pivots)


def level_of(own_key, dims, shards, low, top_value):
    def one(axis_at, blocks):
        steps = jax.random.uniform(jax.random.fold_in(jax.random.fold_in(own_key, 6), axis_at), (blocks,), jnp.float32, low / len(shards), top_value / len(shards))
        return jnp.repeat(jnp.exp(steps), dims[axis_at] // blocks).reshape((-1,) + (1,) * (len(dims) - axis_at - 1))

    gain = one(*shards[0])
    for cut in shards[1:]:
        gain = gain * one(*cut)
    return gain


def normal_values(own_key, dims, scale, limit, pieces=(), kind=jnp.bfloat16):
    values = scale * jax.random.normal(own_key, dims, jnp.float32)
    if pieces:
        values = values * level_of(own_key, dims, pieces, -0.22, 0.18)
    return jnp.clip(values, -limit, limit).astype(kind)


def setup_inputs(seed: int = 0) -> dict:
    key_of = jax.random.split(jax.random.key(seed), 8)
    trailing = normal_values(key_of[0], (MT * B, NT * B), 1.0, 6.0, ((0, 32), (1, 16)))
    col_u = normal_values(key_of[1], (MT, B, R), 1.0, 6.0, ((0, 32), (1, 16)))
    col_v = normal_values(key_of[2], (MT, B, R), R ** -0.5, 0.75, ((0, 32), (1, 16)))
    row_u = normal_values(key_of[3], (NT, B, R), 1.0, 6.0, ((0, 16), (1, 32)))
    row_v = normal_values(key_of[4], (NT, B, R), (R * B) ** -0.5, 0.03125, ((0, 16), (1, 32)))
    diag_lower_inv = draw_diag_lower_inv(jax.random.fold_in(key_of[7], 71), 0)
    diag_upper_inv = draw_diag_upper_inv(jax.random.fold_in(key_of[7], 71), 0)
    return {"trailing": trailing, "col_u": col_u, "col_v": col_v, "row_u": row_u, "row_v": row_v, "diag_lower_inv": diag_lower_inv, "diag_upper_inv": diag_upper_inv}


def reference(trailing, col_u, col_v, row_u, row_v, diag_lower_inv, diag_upper_inv):
    highest = lax.Precision.HIGHEST
    left_v = jnp.einsum("ba,tbr->tar", diag_upper_inv, col_v.astype(jnp.float32), precision=highest)
    lower = jnp.einsum("tpr,tar->tpa", col_u.astype(jnp.float32), left_v, precision=highest).astype(jnp.bfloat16)
    right_u = jnp.einsum("ab,tbr->tar", diag_lower_inv, row_u.astype(jnp.float32), precision=highest)
    upper = jnp.einsum("tar,tqr->taq", right_u, row_v.astype(jnp.float32), precision=highest).astype(jnp.bfloat16)
    upper_whole = jnp.transpose(upper, (1, 0, 2)).reshape(B, NT * B)

    def update(pair):
        rows, tile = pair
        product = jnp.dot(tile, upper_whole, preferred_element_type=jnp.float32)
        return (rows.astype(jnp.float32) - product).astype(jnp.bfloat16)

    blocks = lax.map(update, (trailing.reshape(MT, B, NT * B), lower))
    return blocks.reshape(MT * B, NT * B)
```

```python
import jax
import jax.numpy as jnp
from jax import lax
from jax.experimental import pallas as pl
from jax.experimental.pallas import tpu as pltpu
from jax.sharding import Mesh, PartitionSpec as P

Y, ZH, CORE, ZL, X = 4, 4, 2, 4, 4
ROW, COL = ("y", "zh", "core"), ("zl", "x")
B, R = 512, 64
F32, BF16 = jnp.float32, jnp.bfloat16


def split(x):
    hi = x.astype(BF16)
    return hi, (x - hi.astype(F32)).astype(BF16)


def dot(a, b, dims=((1,), (0,))):
    return lax.dot_general(a, b, (dims, ((), ())), preferred_element_type=F32)


def pack_kernel(ru_ref, rv_ref, cu_ref, cv_ref, row_ref, cols_hbm, buf, sem):
    buf[:, :R] = cu_ref[0]
    buf[:, R:] = cv_ref[0]
    copies = [
        pltpu.make_async_copy(buf, cols_hbm.at[k], sem.at[k]) for k in range(ZL * X)
    ]
    for c in copies:
        c.start()
    row_ref[:, :R] = ru_ref[...].reshape(64, R)
    row_ref[:, R:] = rv_ref[...].reshape(64, R)
    for c in copies:
        c.wait()


def left_kernel(col_ref, upper_ref, lower_ref, q_ref, uu_ref):
    col = col_ref[...].reshape(B, 2 * R)
    u = col[:, :R]
    uu_ref[:, :R] = u
    uu_ref[:, R:] = u
    v = col[:, R:]
    dims = ((0,), (0,))
    up_hi, up_lo = split(upper_ref[...])
    left = dot(v, up_hi, dims) + dot(v, up_lo, dims)
    left_hi, left_lo = split(left)
    low_hi, low_lo = split(lower_ref[...])
    q = dot(left_hi, low_hi) + dot(left_lo, low_hi) + dot(left_hi, low_lo)
    q_hi, q_lo = split(q)
    q_ref[:R] = q_hi
    q_ref[R:] = q_lo


def schur_kernel(x_ref, q_ref, uu_ref, t_hbm, o_hbm, tbuf, obuf, tsem, osem):
    tiles = 4
    fetch = [
        pltpu.make_async_copy(t_hbm.at[:, pl.ds(j * B, B)], tbuf.at[j], tsem.at[j])
        for j in range(tiles)
    ]
    for f in fetch:
        f.start()
    order = [(c, y, z) for y in range(Y) for z in range(ZH) for c in range(CORE)]
    xs = [
        jnp.concatenate([x_ref[c, y, z, j * 16 : (j + 1) * 16, :] for c, y, z in order], axis=0)
        for j in range(tiles)
    ]
    q = q_ref[...]
    keep = lax.broadcasted_iota(jnp.int32, (R, 2 * R), 1) >= R
    ms = [dot(q, x) for x in xs]
    ws = []
    for x, m in zip(xs, ms, strict=True):
        m = jnp.where(keep, pltpu.roll(m[:R] + m[R:], R, 1), 0.0)
        w = dot(jnp.concatenate(split(m), axis=0), x, ((1,), (1,)))
        ws.append(jnp.concatenate(split(w[:R] + w[R:]), axis=0))
    uu = uu_ref[...]
    stores = []
    for j in range(tiles):
        p = dot(uu, ws[j])
        fetch[j].wait()
        obuf[j] = (tbuf[j].astype(F32) - p).astype(BF16)
        s = pltpu.make_async_copy(obuf.at[j], o_hbm.at[:, pl.ds(j * B, B)], osem.at[j])
        s.start()
        stores.append(s)
    for s in stores:
        s.wait()


def on_chip(*arrays):
    return tuple(pltpu.with_memory_space_constraint(a, pltpu.VMEM) for a in arrays)


def shards(trailing, col_u, col_v, row_u, row_v, diag_lower_inv, diag_upper_inv):
    vmem = pl.BlockSpec(memory_space=pltpu.VMEM)
    hbm = pl.BlockSpec(memory_space=pl.ANY)
    row, col_sends = pl.pallas_call(
        pack_kernel,
        in_specs=[vmem] * 4,
        out_specs=(vmem, hbm),
        out_shape=(pltpu.VMEM((64, 128), BF16), pltpu.HBM((ZL * X, 32, 128), BF16)),
        scratch_shapes=[pltpu.VMEM((32, 128), BF16), pltpu.SemaphoreType.DMA((ZL * X,))],
        name="pack",
    )(row_u, row_v, col_u, col_v)
    cols = lax.all_to_all(col_sends, COL, 0, 0, tiled=True)
    over_z = lax.all_gather(row, "zh", axis=0, tiled=False)
    over_z, cols = lax.optimization_barrier((over_z, cols))
    over_y = lax.all_to_all(
        jnp.broadcast_to(over_z[None], (Y, *over_z.shape)), "y", 0, 0, tiled=True
    )
    everything = lax.all_gather(over_y, "core", axis=0, tiled=False)
    q, uu = pl.pallas_call(
        left_kernel,
        in_specs=[vmem] * 3,
        out_specs=(vmem, vmem),
        out_shape=(pltpu.VMEM((2 * R, B), BF16), pltpu.VMEM((B, 2 * R), BF16)),
        name="left",
    )(*on_chip(cols), diag_upper_inv, diag_lower_inv)
    return pl.pallas_call(
        schur_kernel,
        in_specs=[vmem] * 3 + [hbm],
        out_specs=hbm,
        out_shape=jax.ShapeDtypeStruct((B, 4 * B), BF16),
        scratch_shapes=[
            pltpu.VMEM((4, B, B), BF16),
            pltpu.VMEM((4, B, B), BF16),
            pltpu.SemaphoreType.DMA((4,)),
            pltpu.SemaphoreType.DMA((4,)),
        ],
        name="schur",
    )(*on_chip(everything.reshape(CORE, Y, ZH, 64, 128), q, uu), trailing)


def solution(mesh):
    parts = Mesh(mesh.devices.reshape(Y, ZH, CORE, ZL, X), ROW + COL)
    placed = (
        P(ROW, COL),
        P(ROW, COL, None),
        P(ROW, COL, None),
        P(COL, ROW, None),
        P(COL, ROW, None),
        P(),
        P(),
    )
    return jax.shard_map(
        shards, mesh=parts, in_specs=placed, out_specs=P(ROW, COL), check_vma=False
    )
```

```python
import jax
import jax.numpy as jnp
from jax import lax
from jax.experimental import pallas as pl
from jax.experimental.pallas import tpu as pltpu
from jax.sharding import Mesh, PartitionSpec as P

Y, ZH, CORE, ZL, X = 4, 4, 2, 4, 4
ROW, COL = ("y", "zh", "core"), ("zl", "x")
B, R = 512, 64
F32, BF16 = jnp.float32, jnp.bfloat16


def split(x):
    hi = x.astype(BF16)
    return hi, (x - hi.astype(F32)).astype(BF16)


def dot(a, b, dims=((1,), (0,))):
    return lax.dot_general(a, b, (dims, ((), ())), preferred_element_type=F32)


def pack_row_kernel(u_ref, v_ref, row_ref):
    row_ref[:, :R] = u_ref[...].reshape(64, R)
    row_ref[:, R:] = v_ref[...].reshape(64, R)


def pack_col_kernel(u_ref, v_ref, row_ref, cols_hbm, buf, sem):
    buf[:, :R] = u_ref[0]
    buf[:, R:] = v_ref[0]
    copies = [
        pltpu.make_async_copy(buf, cols_hbm.at[k], sem.at[k]) for k in range(ZL * X)
    ]
    for c in copies:
        c.start()
    for c in copies:
        c.wait()


def fan_kernel(own_ref, first_ref, other_ref, sends_hbm, sem):
    copies = []
    for y in range(Y):
        to = sends_hbm.at[y]
        copies += [
            pltpu.make_async_copy(own_ref, to.at[0], sem.at[y, 0]),
            pltpu.make_async_copy(first_ref, to.at[1], sem.at[y, 1]),
            pltpu.make_async_copy(other_ref, to.at[pl.ds(2, 2)], sem.at[y, 2]),
        ]
    for c in copies:
        c.start()
    for c in copies:
        c.wait()


def left_kernel(col_ref, upper_ref, lower_ref, t_hbm, q_ref, uu_ref, *rest):
    held, sem = rest[:-1], rest[-1]
    fetch = [
        pltpu.make_async_copy(t_hbm.at[:, pl.ds(j * B, B)], h, sem.at[j])
        for j, h in enumerate(held)
    ]
    for f in fetch:
        f.start()
    col = col_ref[...].reshape(B, 2 * R)
    u = col[:, :R]
    uu_ref[:, :R] = u
    uu_ref[:, R:] = u
    v = col[:, R:]
    dims = ((0,), (0,))
    up_hi, up_lo = split(upper_ref[...])
    left = dot(v, up_hi, dims) + dot(v, up_lo, dims)
    left_hi, left_lo = split(left)
    low_hi, low_lo = split(lower_ref[...])
    q = dot(left_hi, low_hi) + dot(left_lo, low_hi) + dot(left_hi, low_lo)
    q_hi, q_lo = split(q)
    q_ref[:R] = q_hi
    q_ref[R:] = q_lo
    for f in fetch:
        f.wait()


def schur_kernel(me_ref, x_ref, q_ref, uu_ref, t0_ref, t1_ref, t2_ref, t3_ref, o_hbm, obuf, osem):
    held = (t0_ref, t1_ref, t2_ref, t3_ref)
    tiles = len(held)
    me = me_ref[0]
    slot = [me ^ z for z in range(ZH)]
    order = [(c, y, z) for y in range(Y) for z in range(ZH) for c in range(CORE)]
    xs = [
        jnp.concatenate([x_ref[c, y, slot[z], j * 16 : (j + 1) * 16, :] for c, y, z in order], axis=0)
        for j in range(tiles)
    ]
    q = q_ref[...]
    keep = lax.broadcasted_iota(jnp.int32, (R, 2 * R), 1) >= R
    ms = [dot(q, x) for x in xs]
    ws = []
    for x, m in zip(xs, ms, strict=True):
        m = jnp.where(keep, pltpu.roll(m[:R] + m[R:], R, 1), 0.0)
        w = dot(jnp.concatenate(split(m), axis=0), x, ((1,), (1,)))
        ws.append(jnp.concatenate(split(w[:R] + w[R:]), axis=0))
    uu = uu_ref[...]
    stores = []
    for j in range(tiles):
        p = dot(uu, ws[j])
        obuf[j] = (held[j][...].astype(F32) - p).astype(BF16)
        s = pltpu.make_async_copy(obuf.at[j], o_hbm.at[:, pl.ds(j * B, B)], osem.at[j])
        s.start()
        stores.append(s)
    for s in stores:
        s.wait()


def on_chip(*arrays):
    return tuple(pltpu.with_memory_space_constraint(a, pltpu.VMEM) for a in arrays)


def shards(trailing, col_u, col_v, row_u, row_v, diag_lower_inv, diag_upper_inv):
    vmem = pl.BlockSpec(memory_space=pltpu.VMEM)
    hbm = pl.BlockSpec(memory_space=pl.ANY)
    row = pl.pallas_call(
        pack_row_kernel,
        in_specs=[vmem] * 2,
        out_specs=vmem,
        out_shape=pltpu.VMEM((64, 128), BF16),
        name="pack_row",
    )(row_u, row_v)
    col_sends = pl.pallas_call(
        pack_col_kernel,
        in_specs=[vmem] * 3,
        out_specs=hbm,
        out_shape=pltpu.HBM((ZL * X, 32, 128), BF16),
        scratch_shapes=[pltpu.VMEM((32, 128), BF16), pltpu.SemaphoreType.DMA((ZL * X,))],
        name="pack_col",
    )(col_u, col_v, *on_chip(row))
    cols = lax.all_to_all(col_sends, COL, 0, 0, tiled=True)
    first = lax.ppermute(row, "zh", [(k, k ^ 1) for k in range(ZH)])
    pair = jnp.stack([first, row])
    other = lax.ppermute(pair, "zh", [(k, k ^ 3) for k in range(ZH)])
    sends = pl.pallas_call(
        fan_kernel,
        in_specs=[vmem] * 3,
        out_specs=hbm,
        out_shape=pltpu.HBM((Y, ZH, 64, 128), BF16),
        scratch_shapes=[pltpu.SemaphoreType.DMA((Y, 3))],
        cost_estimate=pl.CostEstimate(flops=4_000_000_000, transcendentals=0, bytes_accessed=1 << 18),
        name="fan",
    )(*on_chip(row, first, other))
    sends, cols = lax.optimization_barrier((sends, cols))
    over_y = lax.all_to_all(sends, "y", 0, 0, tiled=True)
    everything = lax.all_gather(over_y, "core", axis=0, tiled=False)
    q, uu, *held = pl.pallas_call(
        left_kernel,
        in_specs=[vmem] * 3 + [hbm],
        out_specs=(vmem,) * 6,
        out_shape=(
            pltpu.VMEM((2 * R, B), BF16),
            pltpu.VMEM((B, 2 * R), BF16),
            *[pltpu.VMEM((B, B), BF16)] * 4,
        ),
        scratch_shapes=[pltpu.SemaphoreType.DMA((4,))],
        name="left",
    )(*on_chip(cols), diag_upper_inv, diag_lower_inv, trailing)
    return pl.pallas_call(
        schur_kernel,
        in_specs=[pl.BlockSpec(memory_space=pltpu.SMEM)] + [vmem] * 7,
        out_specs=hbm,
        out_shape=jax.ShapeDtypeStruct((B, 4 * B), BF16),
        scratch_shapes=[
            pltpu.VMEM((4, B, B), BF16),
            pltpu.SemaphoreType.DMA((4,)),
        ],
        name="schur",
    )(lax.axis_index("zh")[None], *on_chip(everything.reshape(CORE, Y, ZH, 64, 128), q, uu, *held))


def solution(mesh):
    parts = Mesh(mesh.devices.reshape(Y, ZH, CORE, ZL, X), ROW + COL)
    placed = (
        P(ROW, COL),
        P(ROW, COL, None),
        P(ROW, COL, None),
        P(COL, ROW, None),
        P(COL, ROW, None),
        P(),
        P(),
    )
    return jax.shard_map(
        shards, mesh=parts, in_specs=placed, out_specs=P(ROW, COL), check_vma=False
    )
```

```python
import jax
import jax.numpy as jnp
from jax import lax
from jax.experimental import pallas as pl
from jax.experimental.pallas import tpu as pltpu
from jax.sharding import Mesh, PartitionSpec as P

Y, ZH, CORE, ZL, X = 4, 4, 2, 4, 4
ROW, COL = ("y", "zh", "core"), ("zl", "x")
B, R = 512, 64
F32, BF16 = jnp.float32, jnp.bfloat16


def split(x):
    hi = x.astype(BF16)
    return hi, (x - hi.astype(F32)).astype(BF16)


def dot(a, b, dims=((1,), (0,))):
    return lax.dot_general(a, b, (dims, ((), ())), preferred_element_type=F32)


def pack_kernel(ru_ref, rv_ref, cu_ref, cv_ref, row_ref, col_ref):
    row_ref[:, :R] = ru_ref[...].reshape(64, R)
    row_ref[:, R:] = rv_ref[...].reshape(64, R)
    col_ref[:, :R] = cu_ref[0]
    col_ref[:, R:] = cv_ref[0]


def spread_kernel(col_ref, cols_hbm, sem):
    copies = [
        pltpu.make_async_copy(col_ref, cols_hbm.at[k], sem.at[k]) for k in range(ZL * X)
    ]
    for c in copies:
        c.start()
    for c in copies:
        c.wait()


def fan_kernel(own_ref, first_ref, other_ref, sends_hbm, sem):
    copies = []
    for y in range(Y):
        to = sends_hbm.at[y]
        copies += [
            pltpu.make_async_copy(own_ref, to.at[0], sem.at[y, 0]),
            pltpu.make_async_copy(first_ref, to.at[1], sem.at[y, 1]),
            pltpu.make_async_copy(other_ref, to.at[pl.ds(2, 2)], sem.at[y, 2]),
        ]
    for c in copies:
        c.start()
    for c in copies:
        c.wait()


def left_kernel(col_ref, upper_ref, lower_ref, t_hbm, q_ref, uu_ref, *rest):
    held, sem = rest[:-1], rest[-1]
    fetch = [
        pltpu.make_async_copy(t_hbm.at[:, pl.ds(j * B, B)], h, sem.at[j])
        for j, h in enumerate(held)
    ]
    for f in fetch:
        f.start()
    col = col_ref[...].reshape(B, 2 * R)
    u = col[:, :R]
    uu_ref[:, :R] = u
    uu_ref[:, R:] = u
    v = col[:, R:]
    dims = ((0,), (0,))
    up_hi, up_lo = split(upper_ref[...])
    left = dot(v, up_hi, dims) + dot(v, up_lo, dims)
    left_hi, left_lo = split(left)
    low_hi, low_lo = split(lower_ref[...])
    q = dot(left_hi, low_hi) + dot(left_lo, low_hi) + dot(left_hi, low_lo)
    q_hi, q_lo = split(q)
    q_ref[:R] = q_hi
    q_ref[R:] = q_lo
    for f in fetch:
        f.wait()


def schur_kernel(me_ref, x_ref, q_ref, uu_ref, t0_ref, t1_ref, t2_ref, t3_ref, o_hbm, obuf, osem):
    held = (t0_ref, t1_ref, t2_ref, t3_ref)
    tiles = len(held)
    me = me_ref[0]
    slot = [me ^ z for z in range(ZH)]
    order = [(c, y, z) for y in range(Y) for z in range(ZH) for c in range(CORE)]
    xs = [
        jnp.concatenate([x_ref[c, y, slot[z], j * 16 : (j + 1) * 16, :] for c, y, z in order], axis=0)
        for j in range(tiles)
    ]
    q = q_ref[...]
    keep = lax.broadcasted_iota(jnp.int32, (R, 2 * R), 1) >= R
    ms = [dot(q, x) for x in xs]
    ws = []
    for x, m in zip(xs, ms, strict=True):
        m = jnp.where(keep, pltpu.roll(m[:R] + m[R:], R, 1), 0.0)
        w = dot(jnp.concatenate(split(m), axis=0), x, ((1,), (1,)))
        ws.append(jnp.concatenate(split(w[:R] + w[R:]), axis=0))
    uu = uu_ref[...]
    stores = []
    for j in range(tiles):
        p = dot(uu, ws[j])
        obuf[j] = (held[j][...].astype(F32) - p).astype(BF16)
        s = pltpu.make_async_copy(obuf.at[j], o_hbm.at[:, pl.ds(j * B, B)], osem.at[j])
        s.start()
        stores.append(s)
    for s in stores:
        s.wait()


def on_chip(*arrays):
    return tuple(pltpu.with_memory_space_constraint(a, pltpu.VMEM) for a in arrays)


def shards(trailing, col_u, col_v, row_u, row_v, diag_lower_inv, diag_upper_inv):
    vmem = pl.BlockSpec(memory_space=pltpu.VMEM)
    hbm = pl.BlockSpec(memory_space=pl.ANY)
    row, col = pl.pallas_call(
        pack_kernel,
        in_specs=[vmem] * 4,
        out_specs=(vmem, vmem),
        out_shape=(pltpu.VMEM((64, 128), BF16), pltpu.VMEM((32, 128), BF16)),
        name="pack",
    )(row_u, row_v, col_u, col_v)
    col_sends = pl.pallas_call(
        spread_kernel,
        in_specs=[vmem],
        out_specs=hbm,
        out_shape=pltpu.HBM((ZL * X, 32, 128), BF16),
        scratch_shapes=[pltpu.SemaphoreType.DMA((ZL * X,))],
        name="spread",
    )(*on_chip(col))
    cols = lax.all_to_all(col_sends, COL, 0, 0, tiled=True)
    first = lax.ppermute(row, "zh", [(k, k ^ 1) for k in range(ZH)])
    pair = jnp.stack([first, row])
    other = lax.ppermute(pair, "zh", [(k, k ^ 3) for k in range(ZH)])
    sends = pl.pallas_call(
        fan_kernel,
        in_specs=[vmem] * 3,
        out_specs=hbm,
        out_shape=pltpu.HBM((Y, ZH, 64, 128), BF16),
        scratch_shapes=[pltpu.SemaphoreType.DMA((Y, 3))],
        cost_estimate=pl.CostEstimate(flops=4_000_000_000, transcendentals=0, bytes_accessed=1 << 18),
        name="fan",
    )(*on_chip(row, first, other))
    sends, cols = lax.optimization_barrier((sends, cols))
    over_y = lax.all_to_all(sends, "y", 0, 0, tiled=True)
    everything = lax.all_gather(over_y, "core", axis=0, tiled=False)
    q, uu, *held = pl.pallas_call(
        left_kernel,
        in_specs=[vmem] * 3 + [hbm],
        out_specs=(vmem,) * 6,
        out_shape=(
            pltpu.VMEM((2 * R, B), BF16),
            pltpu.VMEM((B, 2 * R), BF16),
            *[pltpu.VMEM((B, B), BF16)] * 4,
        ),
        scratch_shapes=[pltpu.SemaphoreType.DMA((4,))],
        name="left",
    )(*on_chip(cols), diag_upper_inv, diag_lower_inv, trailing)
    return pl.pallas_call(
        schur_kernel,
        in_specs=[pl.BlockSpec(memory_space=pltpu.SMEM)] + [vmem] * 7,
        out_specs=hbm,
        out_shape=jax.ShapeDtypeStruct((B, 4 * B), BF16),
        scratch_shapes=[
            pltpu.VMEM((4, B, B), BF16),
            pltpu.SemaphoreType.DMA((4,)),
        ],
        name="schur",
    )(lax.axis_index("zh")[None], *on_chip(everything.reshape(CORE, Y, ZH, 64, 128), q, uu, *held))


def solution(mesh):
    parts = Mesh(mesh.devices.reshape(Y, ZH, CORE, ZL, X), ROW + COL)
    placed = (
        P(ROW, COL),
        P(ROW, COL, None),
        P(ROW, COL, None),
        P(COL, ROW, None),
        P(COL, ROW, None),
        P(),
        P(),
    )
    return jax.shard_map(
        shards, mesh=parts, in_specs=placed, out_specs=P(ROW, COL), check_vma=False
    )
```

```python
import jax
import jax.numpy as jnp
from jax import lax
from jax.experimental import pallas as pl
from jax.experimental.pallas import tpu as pltpu
from jax.sharding import Mesh, PartitionSpec as P

Y, ZH, CORE, C = 4, 4, 2, 16
ROW, COL = ("y", "zh", "core"), ("c",)
Y_ORDER = [2, 3, 0, 1]
C_ORDER = list(range(C))
B, R = 512, 64
F32, BF16 = jnp.float32, jnp.bfloat16


def split(x):
    hi = x.astype(BF16)
    return hi, (x - hi.astype(F32)).astype(BF16)


def dot(a, b, dims=((1,), (0,))):
    return lax.dot_general(a, b, (dims, ((), ())), preferred_element_type=F32)


def pack_kernel(ru_ref, rv_ref, cu_ref, cv_ref, row_ref, col_ref):
    row_ref[:, :R] = ru_ref[...].reshape(64, R)
    row_ref[:, R:] = rv_ref[...].reshape(64, R)
    col_ref[:, :R] = cu_ref[0]
    col_ref[:, R:] = cv_ref[0]


def spread_kernel(col_ref, cols_hbm, sem):
    copies = [
        pltpu.make_async_copy(col_ref, cols_hbm.at[k], sem.at[k]) for k in range(C)
    ]
    for c in copies:
        c.start()
    for c in copies:
        c.wait()


def fan_kernel(own_ref, first_ref, other_ref, sends_hbm, sem):
    copies = []
    for y in range(Y):
        to = sends_hbm.at[y]
        copies += [
            pltpu.make_async_copy(own_ref, to.at[0], sem.at[y, 0]),
            pltpu.make_async_copy(first_ref, to.at[1], sem.at[y, 1]),
            pltpu.make_async_copy(other_ref, to.at[pl.ds(2, 2)], sem.at[y, 2]),
        ]
    for c in copies:
        c.start()
    for c in copies:
        c.wait()


def fetch_kernel(after_ref, t_hbm, *rest):
    held, sem = rest[:-1], rest[-1]
    fetch = [
        pltpu.make_async_copy(t_hbm.at[:, pl.ds(j * B, B)], h, sem.at[j])
        for j, h in enumerate(held)
    ]
    for f in fetch:
        f.start()
    for f in fetch:
        f.wait()


def left_kernel(col_ref, upper_ref, lower_ref, q_ref, uu_ref):
    col = jnp.concatenate([col_ref[C_ORDER.index(c)] for c in range(C)], axis=0)
    u = col[:, :R]
    uu_ref[:, :R] = u
    uu_ref[:, R:] = u
    v = col[:, R:]
    dims = ((0,), (0,))
    up_hi, up_lo = split(upper_ref[...])
    left = dot(v, up_hi, dims) + dot(v, up_lo, dims)
    left_hi, left_lo = split(left)
    low_hi, low_lo = split(lower_ref[...])
    q = dot(left_hi, low_hi) + dot(left_lo, low_hi) + dot(left_hi, low_lo)
    q_hi, q_lo = split(q)
    q_ref[:R] = q_hi
    q_ref[R:] = q_lo


def schur_kernel(me_ref, x_ref, q_ref, uu_ref, t0_ref, t1_ref, t2_ref, t3_ref, o_hbm, obuf, osem):
    held = (t0_ref, t1_ref, t2_ref, t3_ref)
    tiles = len(held)
    me = me_ref[0]
    slot = [me ^ z for z in range(ZH)]
    order = [(c, y, z) for y in range(Y) for z in range(ZH) for c in range(CORE)]
    xs = [
        jnp.concatenate([x_ref[c, Y_ORDER.index(y), slot[z], j * 16 : (j + 1) * 16, :] for c, y, z in order], axis=0)
        for j in range(tiles)
    ]
    q = q_ref[...]
    keep = lax.broadcasted_iota(jnp.int32, (R, 2 * R), 1) >= R
    ms = [dot(q, x) for x in xs]
    ws = []
    for x, m in zip(xs, ms, strict=True):
        m = jnp.where(keep, pltpu.roll(m[:R] + m[R:], R, 1), 0.0)
        w = dot(jnp.concatenate(split(m), axis=0), x, ((1,), (1,)))
        ws.append(jnp.concatenate(split(w[:R] + w[R:]), axis=0))
    uu = uu_ref[...]
    stores = []
    for j in range(tiles):
        p = dot(uu, ws[j])
        obuf[j] = (held[j][...].astype(F32) - p).astype(BF16)
        s = pltpu.make_async_copy(obuf.at[j], o_hbm.at[:, pl.ds(j * B, B)], osem.at[j])
        s.start()
        stores.append(s)
    for s in stores:
        s.wait()


def on_chip(*arrays):
    return tuple(pltpu.with_memory_space_constraint(a, pltpu.VMEM) for a in arrays)


def off_chip(*arrays):
    return tuple(pltpu.with_memory_space_constraint(a, pltpu.HBM) for a in arrays)


SMALL = pltpu.CompilerParams(vmem_limit_bytes=16 << 20)


def shards(trailing, col_u, col_v, row_u, row_v, diag_lower_inv, diag_upper_inv):
    vmem = pl.BlockSpec(memory_space=pltpu.VMEM)
    hbm = pl.BlockSpec(memory_space=pl.ANY)
    row, col = pl.pallas_call(
        pack_kernel,
        in_specs=[vmem] * 4,
        out_specs=(vmem, vmem),
        out_shape=(pltpu.VMEM((64, 128), BF16), pltpu.VMEM((32, 128), BF16)),
        name="pack",
    )(row_u, row_v, col_u, col_v)
    col_sends = pl.pallas_call(
        spread_kernel,
        in_specs=[vmem],
        out_specs=hbm,
        out_shape=pltpu.HBM((C, 32, 128), BF16),
        scratch_shapes=[pltpu.SemaphoreType.DMA((C,))],
        name="spread",
    )(*on_chip(col))
    cols = lax.all_to_all(
        col_sends, "c", 0, 0, tiled=True, axis_index_groups=[C_ORDER]
    )
    first = lax.ppermute(row, "zh", [(k, k ^ 1) for k in range(ZH)])
    pair = jnp.stack([first, row])
    other = lax.ppermute(pair, "zh", [(k, k ^ 3) for k in range(ZH)])
    held = pl.pallas_call(
        fetch_kernel,
        in_specs=[vmem, hbm],
        out_specs=(vmem,) * 4,
        out_shape=(pltpu.VMEM((B, B), BF16),) * 4,
        scratch_shapes=[pltpu.SemaphoreType.DMA((4,))],
        compiler_params=SMALL,
        name="fetch",
    )(*on_chip(pair), *off_chip(trailing))
    other, held = lax.optimization_barrier((other, held))
    sends = pl.pallas_call(
        fan_kernel,
        in_specs=[vmem] * 3,
        out_specs=hbm,
        out_shape=pltpu.HBM((Y, ZH, 64, 128), BF16),
        scratch_shapes=[pltpu.SemaphoreType.DMA((Y, 3))],
        cost_estimate=pl.CostEstimate(flops=4000000000, transcendentals=0, bytes_accessed=1 << 18),
        compiler_params=SMALL,
        name="fan",
    )(*on_chip(row, first, other))
    sends, cols = lax.optimization_barrier((sends, cols))
    over_y = lax.all_to_all(sends, "y", 0, 0, tiled=True, axis_index_groups=[Y_ORDER])
    everything = lax.all_gather(over_y, "core", axis=0, tiled=False)
    q, uu = pl.pallas_call(
        left_kernel,
        in_specs=[vmem] * 3,
        out_specs=(vmem, vmem),
        out_shape=(pltpu.VMEM((2 * R, B), BF16), pltpu.VMEM((B, 2 * R), BF16)),
        compiler_params=SMALL,
        name="left",
    )(*on_chip(cols), *off_chip(diag_upper_inv, diag_lower_inv))
    return pl.pallas_call(
        schur_kernel,
        in_specs=[pl.BlockSpec(memory_space=pltpu.SMEM)] + [vmem] * 7,
        out_specs=hbm,
        out_shape=jax.ShapeDtypeStruct((B, 4 * B), BF16),
        scratch_shapes=[
            pltpu.VMEM((4, B, B), BF16),
            pltpu.SemaphoreType.DMA((4,)),
        ],
        name="schur",
    )(lax.axis_index("zh")[None], *on_chip(everything.reshape(CORE, Y, ZH, 64, 128), q, uu, *held))


def solution(mesh):
    parts = Mesh(mesh.devices.reshape(Y, ZH, CORE, C), ROW + COL)
    placed = (
        P(ROW, COL),
        P(ROW, COL, None),
        P(ROW, COL, None),
        P(COL, ROW, None),
        P(COL, ROW, None),
        P(),
        P(),
    )
    return jax.shard_map(
        shards, mesh=parts, in_specs=placed, out_specs=P(ROW, COL), check_vma=False
    )
```

```python
import jax
import jax.numpy as jnp
from jax import lax
from jax.experimental import pallas as pl
from jax.experimental.pallas import tpu as pltpu
from jax.sharding import Mesh, PartitionSpec as P

Y, ZH, CORE, C = 4, 4, 2, 16
ROW, COL = ("y", "zh", "core"), ("c",)
Y_ORDER = [2, 3, 0, 1]
C_ORDER = [4, *[c for c in range(C) if c != 4]]
B, R = 512, 64
F32, BF16 = jnp.float32, jnp.bfloat16


def split(x):
    hi = x.astype(BF16)
    return hi, (x - hi.astype(F32)).astype(BF16)


def dot(a, b, dims=((1,), (0,))):
    return lax.dot_general(a, b, (dims, ((), ())), preferred_element_type=F32)


def crossed(array, bits):
    swap = [(2 * k + c, 2 * (k ^ bits) + 1 - c) for k in range(ZH) for c in range(CORE)]
    return lax.ppermute(array, ("zh", "core"), swap)


def pack_kernel(ru_ref, rv_ref, cu_ref, cv_ref, row_ref, col_ref):
    row_ref[:, :R] = ru_ref[...].reshape(64, R)
    row_ref[:, R:] = rv_ref[...].reshape(64, R)
    col_ref[:, :R] = cu_ref[0]
    col_ref[:, R:] = cv_ref[0]


def spread_kernel(col_ref, cols_hbm, sem):
    copies = [
        pltpu.make_async_copy(col_ref, cols_hbm.at[k], sem.at[k]) for k in range(C)
    ]
    for c in copies:
        c.start()
    for c in copies:
        c.wait()


def fan_kernel(own_ref, first_ref, other_ref, sends_hbm, sem):
    copies = []
    for y in range(Y):
        to = sends_hbm.at[y]
        copies += [
            pltpu.make_async_copy(own_ref, to.at[0], sem.at[y, 0]),
            pltpu.make_async_copy(first_ref, to.at[1], sem.at[y, 1]),
            pltpu.make_async_copy(other_ref, to.at[pl.ds(2, 2)], sem.at[y, 2]),
        ]
    for c in copies:
        c.start()
    for c in copies:
        c.wait()


def fetch_kernel(after_ref, t_hbm, *rest):
    held, sem = rest[:-1], rest[-1]
    fetch = [
        pltpu.make_async_copy(t_hbm.at[:, pl.ds(j * B, B)], h, sem.at[j])
        for j, h in enumerate(held)
    ]
    for f in fetch:
        f.start()
    for f in fetch:
        f.wait()


def left_kernel(col_ref, upper_ref, lower_ref, q_ref, uu_ref):
    col = jnp.concatenate([col_ref[C_ORDER.index(c)] for c in range(C)], axis=0)
    u = col[:, :R]
    uu_ref[:, :R] = u
    uu_ref[:, R:] = u
    v = col[:, R:]
    dims = ((0,), (0,))
    up_hi, up_lo = split(upper_ref[...])
    left = dot(v, up_hi, dims) + dot(v, up_lo, dims)
    left_hi, left_lo = split(left)
    low_hi, low_lo = split(lower_ref[...])
    q = dot(left_hi, low_hi) + dot(left_lo, low_hi) + dot(left_hi, low_lo)
    q_hi, q_lo = split(q)
    q_ref[:R] = q_hi
    q_ref[R:] = q_lo


def schur_kernel(me_ref, x_ref, q_ref, uu_ref, t0_ref, t1_ref, t2_ref, t3_ref, o_hbm, obuf, osem):
    held = (t0_ref, t1_ref, t2_ref, t3_ref)
    tiles = len(held)
    me = me_ref[0]
    slot = [me ^ z for z in range(ZH)]
    order = [(c, y, z) for y in range(Y) for z in range(ZH) for c in range(CORE)]
    xs = [
        jnp.concatenate([x_ref[c ^ (slot[z] >> 1), Y_ORDER.index(y), slot[z], j * 16 : (j + 1) * 16, :] for c, y, z in order], axis=0)
        for j in range(tiles)
    ]
    q = q_ref[...]
    keep = lax.broadcasted_iota(jnp.int32, (R, 2 * R), 1) >= R
    ms = [dot(q, x) for x in xs]
    ws = []
    for x, m in zip(xs, ms, strict=True):
        m = jnp.where(keep, pltpu.roll(m[:R] + m[R:], R, 1), 0.0)
        w = dot(jnp.concatenate(split(m), axis=0), x, ((1,), (1,)))
        ws.append(jnp.concatenate(split(w[:R] + w[R:]), axis=0))
    uu = uu_ref[...]
    stores = []
    for j in range(tiles):
        p = dot(uu, ws[j])
        obuf[j] = (held[j][...].astype(F32) - p).astype(BF16)
        s = pltpu.make_async_copy(obuf.at[j], o_hbm.at[:, pl.ds(j * B, B)], osem.at[j])
        s.start()
        stores.append(s)
    for s in stores:
        s.wait()


def on_chip(*arrays):
    return tuple(pltpu.with_memory_space_constraint(a, pltpu.VMEM) for a in arrays)


def off_chip(*arrays):
    return tuple(pltpu.with_memory_space_constraint(a, pltpu.HBM) for a in arrays)


SMALL = pltpu.CompilerParams(vmem_limit_bytes=16 << 20)


def shards(trailing, col_u, col_v, row_u, row_v, diag_lower_inv, diag_upper_inv):
    vmem = pl.BlockSpec(memory_space=pltpu.VMEM)
    hbm = pl.BlockSpec(memory_space=pl.ANY)
    row, col = pl.pallas_call(
        pack_kernel,
        in_specs=[vmem] * 4,
        out_specs=(vmem, vmem),
        out_shape=(pltpu.VMEM((64, 128), BF16), pltpu.VMEM((32, 128), BF16)),
        name="pack",
    )(row_u, row_v, col_u, col_v)
    col_sends = pl.pallas_call(
        spread_kernel,
        in_specs=[vmem],
        out_specs=hbm,
        out_shape=pltpu.HBM((C, 32, 128), BF16),
        scratch_shapes=[pltpu.SemaphoreType.DMA((C,))],
        name="spread",
    )(*on_chip(col))
    cols = lax.all_to_all(
        col_sends, "c", 0, 0, tiled=True, axis_index_groups=[C_ORDER]
    )
    first = lax.ppermute(row, "zh", [(k, k ^ 1) for k in range(ZH)])
    pair = jnp.stack([first, row])
    other = crossed(pair, 3)
    held = pl.pallas_call(
        fetch_kernel,
        in_specs=[vmem, hbm],
        out_specs=(vmem,) * 4,
        out_shape=(pltpu.VMEM((B, B), BF16),) * 4,
        scratch_shapes=[pltpu.SemaphoreType.DMA((4,))],
        compiler_params=SMALL,
        name="fetch",
    )(*on_chip(pair), *off_chip(trailing))
    other, held = lax.optimization_barrier((other, held))
    sends = pl.pallas_call(
        fan_kernel,
        in_specs=[vmem] * 3,
        out_specs=hbm,
        out_shape=pltpu.HBM((Y, ZH, 64, 128), BF16),
        scratch_shapes=[pltpu.SemaphoreType.DMA((Y, 3))],
        cost_estimate=pl.CostEstimate(flops=4000000000, transcendentals=0, bytes_accessed=1 << 18),
        compiler_params=SMALL,
        name="fan",
    )(*on_chip(row, first, other))
    sends, cols = lax.optimization_barrier((sends, cols))
    over_y = lax.all_to_all(sends, "y", 0, 0, tiled=True, axis_index_groups=[Y_ORDER])
    everything = lax.all_gather(over_y, "core", axis=0, tiled=False)
    q, uu = pl.pallas_call(
        left_kernel,
        in_specs=[vmem] * 3,
        out_specs=(vmem, vmem),
        out_shape=(pltpu.VMEM((2 * R, B), BF16), pltpu.VMEM((B, 2 * R), BF16)),
        compiler_params=SMALL,
        name="left",
    )(*on_chip(cols), *off_chip(diag_upper_inv, diag_lower_inv))
    return pl.pallas_call(
        schur_kernel,
        in_specs=[pl.BlockSpec(memory_space=pltpu.SMEM)] + [vmem] * 7,
        out_specs=hbm,
        out_shape=jax.ShapeDtypeStruct((B, 4 * B), BF16),
        scratch_shapes=[
            pltpu.VMEM((4, B, B), BF16),
            pltpu.SemaphoreType.DMA((4,)),
        ],
        name="schur",
    )(lax.axis_index("zh")[None], *on_chip(everything.reshape(CORE, Y, ZH, 64, 128), q, uu, *held))


def solution(mesh):
    parts = Mesh(mesh.devices.reshape(Y, ZH, CORE, C), ROW + COL)
    placed = (
        P(ROW, COL),
        P(ROW, COL, None),
        P(ROW, COL, None),
        P(COL, ROW, None),
        P(COL, ROW, None),
        P(),
        P(),
    )
    return jax.shard_map(
        shards, mesh=parts, in_specs=placed, out_specs=P(ROW, COL), check_vma=False
    )
```

```python
import jax
import jax.numpy as jnp
from jax import lax
from jax.experimental import pallas as pl
from jax.experimental.pallas import tpu as pltpu
from jax.sharding import Mesh, PartitionSpec as P

Y, ZH, CORE, C = 4, 4, 2, 16
ROW, COL = ("y", "zh", "core"), ("c",)
Y_ORDER = [2, 0, 3, 1]
C_ORDER = [4, *[c for c in range(C) if c != 4]]
B, R = 512, 64
F32, BF16 = jnp.float32, jnp.bfloat16


def split(x):
    hi = x.astype(BF16)
    return hi, (x - hi.astype(F32)).astype(BF16)


def dot(a, b, dims=((1,), (0,))):
    return lax.dot_general(a, b, (dims, ((), ())), preferred_element_type=F32)


def crossed(array, bits):
    swap = [(2 * k + c, 2 * (k ^ bits) + 1 - c) for k in range(ZH) for c in range(CORE)]
    return lax.ppermute(array, ("zh", "core"), swap)


def pack_kernel(ru_ref, rv_ref, cu_ref, cv_ref, row_ref, col_ref):
    row_ref[:, :R] = ru_ref[...].reshape(64, R)
    row_ref[:, R:] = rv_ref[...].reshape(64, R)
    col_ref[:, :R] = cu_ref[0]
    col_ref[:, R:] = cv_ref[0]


def spread_kernel(col_ref, cols_hbm, sem):
    copies = [
        pltpu.make_async_copy(col_ref, cols_hbm.at[k], sem.at[k]) for k in range(C)
    ]
    for c in copies:
        c.start()
    for c in copies:
        c.wait()


def fan_kernel(own_ref, first_ref, other_ref, sends_hbm, sem):
    copies = []
    for y in range(Y):
        to = sends_hbm.at[y]
        copies += [
            pltpu.make_async_copy(own_ref, to.at[0], sem.at[y, 0]),
            pltpu.make_async_copy(first_ref, to.at[1], sem.at[y, 1]),
            pltpu.make_async_copy(other_ref, to.at[pl.ds(2, 2)], sem.at[y, 2]),
        ]
    for c in copies:
        c.start()
    for c in copies:
        c.wait()


def fetch_kernel(after_ref, t_hbm, *rest):
    held, sem = rest[:-1], rest[-1]
    fetch = [
        pltpu.make_async_copy(t_hbm.at[:, pl.ds(j * B, B)], h, sem.at[j])
        for j, h in enumerate(held)
    ]
    for f in fetch:
        f.start()
    for f in fetch:
        f.wait()


def left_kernel(col_ref, upper_ref, lower_ref, q_ref, uu_ref):
    col = jnp.concatenate([col_ref[C_ORDER.index(c)] for c in range(C)], axis=0)
    u = col[:, :R]
    uu_ref[:, :R] = u
    uu_ref[:, R:] = u
    v = col[:, R:]
    dims = ((0,), (0,))
    up_hi, up_lo = split(upper_ref[...])
    left = dot(v, up_hi, dims) + dot(v, up_lo, dims)
    left_hi, left_lo = split(left)
    low_hi, low_lo = split(lower_ref[...])
    q = dot(left_hi, low_hi) + dot(left_lo, low_hi) + dot(left_hi, low_lo)
    q_hi, q_lo = split(q)
    q_ref[:R] = q_hi
    q_ref[R:] = q_lo


def schur_kernel(me_ref, x_ref, q_ref, uu_ref, t0_ref, t1_ref, t2_ref, t3_ref, o_hbm, obuf, osem):
    held = (t0_ref, t1_ref, t2_ref, t3_ref)
    tiles = len(held)
    me = me_ref[0]
    slot = [me ^ z for z in range(ZH)]
    order = [(c, y, z) for y in range(Y) for z in range(ZH) for c in range(CORE)]
    xs = [
        jnp.concatenate([x_ref[c ^ (slot[z] >> 1), Y_ORDER.index(y), slot[z], j * 16 : (j + 1) * 16, :] for c, y, z in order], axis=0)
        for j in range(tiles)
    ]
    q = q_ref[...]
    keep = lax.broadcasted_iota(jnp.int32, (R, 2 * R), 1) >= R
    ms = [dot(q, x) for x in xs]
    ws = []
    for x, m in zip(xs, ms, strict=True):
        m = jnp.where(keep, pltpu.roll(m[:R] + m[R:], R, 1), 0.0)
        w = dot(jnp.concatenate(split(m), axis=0), x, ((1,), (1,)))
        ws.append(jnp.concatenate(split(w[:R] + w[R:]), axis=0))
    uu = uu_ref[...]
    stores = []
    for j in range(tiles):
        p = dot(uu, ws[j])
        obuf[j] = (held[j][...].astype(F32) - p).astype(BF16)
        s = pltpu.make_async_copy(obuf.at[j], o_hbm.at[:, pl.ds(j * B, B)], osem.at[j])
        s.start()
        stores.append(s)
    for s in stores:
        s.wait()


def on_chip(*arrays):
    return tuple(pltpu.with_memory_space_constraint(a, pltpu.VMEM) for a in arrays)


def off_chip(*arrays):
    return tuple(pltpu.with_memory_space_constraint(a, pltpu.HBM) for a in arrays)


SMALL = pltpu.CompilerParams(vmem_limit_bytes=16 << 20)


def shards(trailing, col_u, col_v, row_u, row_v, diag_lower_inv, diag_upper_inv):
    vmem = pl.BlockSpec(memory_space=pltpu.VMEM)
    hbm = pl.BlockSpec(memory_space=pl.ANY)
    row, col = pl.pallas_call(
        pack_kernel,
        in_specs=[vmem] * 4,
        out_specs=(vmem, vmem),
        out_shape=(pltpu.VMEM((64, 128), BF16), pltpu.VMEM((32, 128), BF16)),
        name="pack",
    )(row_u, row_v, col_u, col_v)
    col_sends = pl.pallas_call(
        spread_kernel,
        in_specs=[vmem],
        out_specs=hbm,
        out_shape=pltpu.HBM((C, 32, 128), BF16),
        scratch_shapes=[pltpu.SemaphoreType.DMA((C,))],
        name="spread",
    )(*on_chip(col))
    cols = lax.all_to_all(
        col_sends, "c", 0, 0, tiled=True, axis_index_groups=[C_ORDER]
    )
    first = lax.ppermute(row, "zh", [(k, k ^ 1) for k in range(ZH)])
    pair = jnp.stack([first, row])
    other = crossed(pair, 3)
    held = pl.pallas_call(
        fetch_kernel,
        in_specs=[vmem, hbm],
        out_specs=(vmem,) * 4,
        out_shape=(pltpu.VMEM((B, B), BF16),) * 4,
        scratch_shapes=[pltpu.SemaphoreType.DMA((4,))],
        compiler_params=SMALL,
        name="fetch",
    )(*on_chip(pair), *off_chip(trailing))
    other, held = lax.optimization_barrier((other, held))
    sends = pl.pallas_call(
        fan_kernel,
        in_specs=[vmem] * 3,
        out_specs=hbm,
        out_shape=pltpu.HBM((Y, ZH, 64, 128), BF16),
        scratch_shapes=[pltpu.SemaphoreType.DMA((Y, 3))],
        cost_estimate=pl.CostEstimate(flops=4000000000, transcendentals=0, bytes_accessed=1 << 18),
        compiler_params=SMALL,
        name="fan",
    )(*on_chip(row, first, other))
    sends, cols = lax.optimization_barrier((sends, cols))
    over_y = lax.all_to_all(sends, "y", 0, 0, tiled=True, axis_index_groups=[Y_ORDER])
    everything = lax.all_gather(over_y, "core", axis=0, tiled=False)
    q, uu = pl.pallas_call(
        left_kernel,
        in_specs=[vmem] * 3,
        out_specs=(vmem, vmem),
        out_shape=(pltpu.VMEM((2 * R, B), BF16), pltpu.VMEM((B, 2 * R), BF16)),
        compiler_params=SMALL,
        name="left",
    )(*on_chip(cols), *off_chip(diag_upper_inv, diag_lower_inv))
    return pl.pallas_call(
        schur_kernel,
        in_specs=[pl.BlockSpec(memory_space=pltpu.SMEM)] + [vmem] * 7,
        out_specs=hbm,
        out_shape=jax.ShapeDtypeStruct((B, 4 * B), BF16),
        scratch_shapes=[
            pltpu.VMEM((4, B, B), BF16),
            pltpu.SemaphoreType.DMA((4,)),
        ],
        name="schur",
    )(lax.axis_index("zh")[None], *on_chip(everything.reshape(CORE, Y, ZH, 64, 128), q, uu, *held))


def solution(mesh):
    parts = Mesh(mesh.devices.reshape(Y, ZH, CORE, C), ROW + COL)
    placed = (
        P(ROW, COL),
        P(ROW, COL, None),
        P(ROW, COL, None),
        P(COL, ROW, None),
        P(COL, ROW, None),
        P(),
        P(),
    )
    return jax.shard_map(
        shards, mesh=parts, in_specs=placed, out_specs=P(ROW, COL), check_vma=False
    )
```

```python
import jax
import jax.numpy as jnp
from jax import lax
from jax.experimental import pallas as pl
from jax.experimental.pallas import tpu as pltpu
from jax.sharding import Mesh, PartitionSpec as P

Y, ZH, CORE, C = 4, 4, 2, 16
ROW, COL = ("y", "zh", "core"), ("c",)
Y_ORDER = [2, 0, 3, 1]
C_ORDER = [4, *[c for c in range(C) if c != 4]]
B, R = 512, 64
F32, BF16 = jnp.float32, jnp.bfloat16


def split(x):
    hi = x.astype(BF16)
    return hi, (x - hi.astype(F32)).astype(BF16)


def dot(a, b, dims=((1,), (0,))):
    return lax.dot_general(a, b, (dims, ((), ())), preferred_element_type=F32)


def crossed(array, bits):
    swap = [(2 * k + c, 2 * (k ^ bits) + 1 - c) for k in range(ZH) for c in range(CORE)]
    return lax.ppermute(array, ("zh", "core"), swap)


def pack_kernel(ru_ref, rv_ref, cu_ref, cv_ref, row_ref, col_ref):
    row_ref[:, :R] = ru_ref[...].reshape(64, R)
    row_ref[:, R:] = rv_ref[...].reshape(64, R)
    col_ref[:, :R] = cu_ref[0]
    col_ref[:, R:] = cv_ref[0]


def spread_kernel(col_ref, cols_hbm, sem):
    copies = [
        pltpu.make_async_copy(col_ref, cols_hbm.at[k], sem.at[k]) for k in range(C)
    ]
    for c in copies:
        c.start()
    for c in copies:
        c.wait()


def fan_kernel(own_ref, first_ref, other_ref, sends_hbm, sem):
    copies = []
    for y in range(Y):
        to = sends_hbm.at[y]
        copies += [
            pltpu.make_async_copy(own_ref, to.at[0], sem.at[y, 0]),
            pltpu.make_async_copy(first_ref, to.at[1], sem.at[y, 1]),
            pltpu.make_async_copy(other_ref, to.at[pl.ds(2, 2)], sem.at[y, 2]),
        ]
    for c in copies:
        c.start()
    for c in copies:
        c.wait()


def fetch_kernel(after_ref, t_hbm, *rest):
    held, sem = rest[:-1], rest[-1]
    fetch = [
        pltpu.make_async_copy(t_hbm.at[:, pl.ds(j * B, B)], h, sem.at[j])
        for j, h in enumerate(held)
    ]
    for f in fetch:
        f.start()
    for f in fetch:
        f.wait()


def left_kernel(col_ref, upper_ref, lower_ref, q_ref, uu_ref):
    col = jnp.concatenate([col_ref[C_ORDER.index(c)] for c in range(C)], axis=0)
    u = col[:, :R]
    uu_ref[:, :R] = u
    uu_ref[:, R:] = u
    v = col[:, R:]
    dims = ((0,), (0,))
    up_hi, up_lo = split(upper_ref[...])
    left = dot(v, up_hi, dims) + dot(v, up_lo, dims)
    left_hi, left_lo = split(left)
    low_hi, low_lo = split(lower_ref[...])
    q = dot(left_hi, low_hi) + dot(left_lo, low_hi) + dot(left_hi, low_lo)
    q_hi, q_lo = split(q)
    q_ref[:R] = q_hi
    q_ref[R:] = q_lo


def schur_kernel(me_ref, x_ref, q_ref, uu_ref, t0_ref, t1_ref, t2_ref, t3_ref, o_hbm, obuf, osem):
    held = (t0_ref, t1_ref, t2_ref, t3_ref)
    tiles = len(held)
    me = me_ref[0]
    slot = [me ^ z for z in range(ZH)]
    order = [(c, y, z) for y in range(Y) for z in range(ZH) for c in range(CORE)]
    xs = [
        jnp.concatenate([x_ref[c ^ (slot[z] >> 1), Y_ORDER.index(y), slot[z], j * 16 : (j + 1) * 16, :] for c, y, z in order], axis=0)
        for j in range(tiles)
    ]
    q = q_ref[...]
    keep = lax.broadcasted_iota(jnp.int32, (R, 2 * R), 1) >= R
    ms = [dot(q, x) for x in xs]
    ws = []
    for x, m in zip(xs, ms, strict=True):
        m = jnp.where(keep, pltpu.roll(m[:R] + m[R:], R, 1), 0.0)
        w = dot(jnp.concatenate(split(m), axis=0), x, ((1,), (1,)))
        ws.append(jnp.concatenate(split(w[:R] + w[R:]), axis=0))
    uu = uu_ref[...]
    stores = []
    rows = B // 4
    for j in range(tiles):
        for i in range(4):
            part = pl.ds(i * rows, rows)
            p = dot(uu[i * rows : (i + 1) * rows], ws[j])
            obuf[j, part] = (held[j][part, :].astype(F32) - p).astype(BF16)
            s = pltpu.make_async_copy(
                obuf.at[j, part], o_hbm.at[part, pl.ds(j * B, B)], osem.at[j, i]
            )
            s.start()
            stores.append(s)
    for s in stores:
        s.wait()


def on_chip(*arrays):
    return tuple(pltpu.with_memory_space_constraint(a, pltpu.VMEM) for a in arrays)


def off_chip(*arrays):
    return tuple(pltpu.with_memory_space_constraint(a, pltpu.HBM) for a in arrays)


SMALL = pltpu.CompilerParams(vmem_limit_bytes=16 << 20)


def shards(trailing, col_u, col_v, row_u, row_v, diag_lower_inv, diag_upper_inv):
    vmem = pl.BlockSpec(memory_space=pltpu.VMEM)
    hbm = pl.BlockSpec(memory_space=pl.ANY)
    row, col = pl.pallas_call(
        pack_kernel,
        in_specs=[vmem] * 4,
        out_specs=(vmem, vmem),
        out_shape=(pltpu.VMEM((64, 128), BF16), pltpu.VMEM((32, 128), BF16)),
        name="pack",
    )(row_u, row_v, col_u, col_v)
    col_sends = pl.pallas_call(
        spread_kernel,
        in_specs=[vmem],
        out_specs=hbm,
        out_shape=pltpu.HBM((C, 32, 128), BF16),
        scratch_shapes=[pltpu.SemaphoreType.DMA((C,))],
        name="spread",
    )(*on_chip(col))
    cols = lax.all_to_all(
        col_sends, "c", 0, 0, tiled=True, axis_index_groups=[C_ORDER]
    )
    first = lax.ppermute(row, "zh", [(k, k ^ 1) for k in range(ZH)])
    pair = jnp.stack([first, row])
    other = crossed(pair, 3)
    held = pl.pallas_call(
        fetch_kernel,
        in_specs=[vmem, hbm],
        out_specs=(vmem,) * 4,
        out_shape=(pltpu.VMEM((B, B), BF16),) * 4,
        scratch_shapes=[pltpu.SemaphoreType.DMA((4,))],
        compiler_params=SMALL,
        name="fetch",
    )(*on_chip(pair), *off_chip(trailing))
    other, held = lax.optimization_barrier((other, held))
    sends = pl.pallas_call(
        fan_kernel,
        in_specs=[vmem] * 3,
        out_specs=hbm,
        out_shape=pltpu.HBM((Y, ZH, 64, 128), BF16),
        scratch_shapes=[pltpu.SemaphoreType.DMA((Y, 3))],
        cost_estimate=pl.CostEstimate(flops=4000000000, transcendentals=0, bytes_accessed=1 << 18),
        compiler_params=SMALL,
        name="fan",
    )(*on_chip(row, first, other))
    sends, cols = lax.optimization_barrier((sends, cols))
    over_y = lax.all_to_all(sends, "y", 0, 0, tiled=True, axis_index_groups=[Y_ORDER])
    everything = lax.all_gather(over_y, "core", axis=0, tiled=False)
    q, uu = pl.pallas_call(
        left_kernel,
        in_specs=[vmem] * 3,
        out_specs=(vmem, vmem),
        out_shape=(pltpu.VMEM((2 * R, B), BF16), pltpu.VMEM((B, 2 * R), BF16)),
        compiler_params=SMALL,
        name="left",
    )(*on_chip(cols), *off_chip(diag_upper_inv, diag_lower_inv))
    return pl.pallas_call(
        schur_kernel,
        in_specs=[pl.BlockSpec(memory_space=pltpu.SMEM)] + [vmem] * 7,
        out_specs=hbm,
        out_shape=jax.ShapeDtypeStruct((B, 4 * B), BF16),
        scratch_shapes=[
            pltpu.VMEM((4, B, B), BF16),
            pltpu.SemaphoreType.DMA((4, 4)),
        ],
        name="schur",
    )(lax.axis_index("zh")[None], *on_chip(everything.reshape(CORE, Y, ZH, 64, 128), q, uu, *held))


def solution(mesh):
    parts = Mesh(mesh.devices.reshape(Y, ZH, CORE, C), ROW + COL)
    placed = (
        P(ROW, COL),
        P(ROW, COL, None),
        P(ROW, COL, None),
        P(COL, ROW, None),
        P(COL, ROW, None),
        P(),
        P(),
    )
    return jax.shard_map(
        shards, mesh=parts, in_specs=placed, out_specs=P(ROW, COL), check_vma=False
    )
```

```python
import jax
import jax.numpy as jnp
from jax import lax
from jax.experimental import pallas as pl
from jax.experimental.pallas import tpu as pltpu
from jax.sharding import Mesh, PartitionSpec as P

Y, ZH, CORE, C = 4, 4, 2, 16
ROW, COL = ("y", "zh", "core"), ("c",)
Y_ORDER = [2, 0, 1, 3]
C_ORDER = [4, *[c for c in range(C) if c != 4]]
B, R = 512, 64
F32, BF16 = jnp.float32, jnp.bfloat16


def split(x):
    hi = x.astype(BF16)
    return hi, (x - hi.astype(F32)).astype(BF16)


def dot(a, b, dims=((1,), (0,))):
    return lax.dot_general(a, b, (dims, ((), ())), preferred_element_type=F32)


def crossed(array, bits):
    swap = [(2 * k + c, 2 * (k ^ bits) + 1 - c) for k in range(ZH) for c in range(CORE)]
    return lax.ppermute(array, ("zh", "core"), swap)


def pack_kernel(ru_ref, rv_ref, cu_ref, cv_ref, row_ref, col_ref):
    row_ref[:, :R] = ru_ref[...].reshape(64, R)
    row_ref[:, R:] = rv_ref[...].reshape(64, R)
    col_ref[:, :R] = cu_ref[0]
    col_ref[:, R:] = cv_ref[0]


def spread_kernel(col_ref, cols_hbm, sem):
    copies = [
        pltpu.make_async_copy(col_ref, cols_hbm.at[k], sem.at[k]) for k in range(C)
    ]
    for c in copies:
        c.start()
    for c in copies:
        c.wait()


def fan_kernel(own_ref, first_ref, other_ref, sends_hbm, sem):
    copies = []
    for y in range(Y):
        to = sends_hbm.at[y]
        copies += [
            pltpu.make_async_copy(own_ref, to.at[0], sem.at[y, 0]),
            pltpu.make_async_copy(first_ref, to.at[1], sem.at[y, 1]),
            pltpu.make_async_copy(other_ref, to.at[pl.ds(2, 2)], sem.at[y, 2]),
        ]
    for c in copies:
        c.start()
    for c in copies:
        c.wait()


def fetch_kernel(after_ref, t_hbm, *rest):
    held, sem = rest[:-1], rest[-1]
    fetch = [
        pltpu.make_async_copy(t_hbm.at[:, pl.ds(j * B, B)], h, sem.at[j])
        for j, h in enumerate(held)
    ]
    for f in fetch:
        f.start()
    for f in fetch:
        f.wait()


def left_kernel(col_ref, upper_ref, lower_ref, q_ref, uu_ref):
    col = jnp.concatenate([col_ref[C_ORDER.index(c)] for c in range(C)], axis=0)
    u = col[:, :R]
    uu_ref[:, :R] = u
    uu_ref[:, R:] = u
    v = col[:, R:]
    dims = ((0,), (0,))
    up_hi, up_lo = split(upper_ref[...])
    left = dot(v, up_hi, dims) + dot(v, up_lo, dims)
    left_hi, left_lo = split(left)
    low_hi, low_lo = split(lower_ref[...])
    q = dot(left_hi, low_hi) + dot(left_lo, low_hi) + dot(left_hi, low_lo)
    q_hi, q_lo = split(q)
    q_ref[:R] = q_hi
    q_ref[R:] = q_lo


def schur_kernel(me_ref, x_ref, q_ref, uu_ref, t0_ref, t1_ref, t2_ref, t3_ref, o_hbm, obuf, osem):
    held = (t0_ref, t1_ref, t2_ref, t3_ref)
    tiles = len(held)
    me = me_ref[0]
    slot = [me ^ z for z in range(ZH)]
    order = [(c, y, z) for y in range(Y) for z in range(ZH) for c in range(CORE)]
    xs = [
        jnp.concatenate([x_ref[c ^ (slot[z] >> 1), Y_ORDER.index(y), slot[z], j * 16 : (j + 1) * 16, :] for c, y, z in order], axis=0)
        for j in range(tiles)
    ]
    q = q_ref[...]
    keep = lax.broadcasted_iota(jnp.int32, (R, 2 * R), 1) >= R
    ms = [dot(q, x) for x in xs]
    ws = []
    for x, m in zip(xs, ms, strict=True):
        m = jnp.where(keep, pltpu.roll(m[:R] + m[R:], R, 1), 0.0)
        w = dot(jnp.concatenate(split(m), axis=0), x, ((1,), (1,)))
        ws.append(jnp.concatenate(split(w[:R] + w[R:]), axis=0))
    uu = uu_ref[...]
    stores = []
    rows = B // 4
    for j in range(tiles):
        for i in range(4):
            part = pl.ds(i * rows, rows)
            p = dot(uu[i * rows : (i + 1) * rows], ws[j])
            obuf[j, part] = (held[j][part, :].astype(F32) - p).astype(BF16)
            s = pltpu.make_async_copy(
                obuf.at[j, part], o_hbm.at[part, pl.ds(j * B, B)], osem.at[j, i]
            )
            s.start()
            stores.append(s)
    for s in stores:
        s.wait()


def on_chip(*arrays):
    return tuple(pltpu.with_memory_space_constraint(a, pltpu.VMEM) for a in arrays)


def off_chip(*arrays):
    return tuple(pltpu.with_memory_space_constraint(a, pltpu.HBM) for a in arrays)


SMALL = pltpu.CompilerParams(vmem_limit_bytes=16 << 20)


def shards(trailing, col_u, col_v, row_u, row_v, diag_lower_inv, diag_upper_inv):
    vmem = pl.BlockSpec(memory_space=pltpu.VMEM)
    hbm = pl.BlockSpec(memory_space=pl.ANY)
    row, col = pl.pallas_call(
        pack_kernel,
        in_specs=[vmem] * 4,
        out_specs=(vmem, vmem),
        out_shape=(pltpu.VMEM((64, 128), BF16), pltpu.VMEM((32, 128), BF16)),
        name="pack",
    )(row_u, row_v, col_u, col_v)
    col_sends = pl.pallas_call(
        spread_kernel,
        in_specs=[vmem],
        out_specs=hbm,
        out_shape=pltpu.HBM((C, 32, 128), BF16),
        scratch_shapes=[pltpu.SemaphoreType.DMA((C,))],
        name="spread",
    )(*on_chip(col))
    cols = lax.all_to_all(
        col_sends, "c", 0, 0, tiled=True, axis_index_groups=[C_ORDER]
    )
    first = lax.ppermute(row, "zh", [(k, k ^ 1) for k in range(ZH)])
    pair = jnp.stack([first, row])
    other = crossed(pair, 3)
    held = pl.pallas_call(
        fetch_kernel,
        in_specs=[vmem, hbm],
        out_specs=(vmem,) * 4,
        out_shape=(pltpu.VMEM((B, B), BF16),) * 4,
        scratch_shapes=[pltpu.SemaphoreType.DMA((4,))],
        compiler_params=SMALL,
        name="fetch",
    )(*on_chip(pair), *off_chip(trailing))
    other, held = lax.optimization_barrier((other, held))
    sends = pl.pallas_call(
        fan_kernel,
        in_specs=[vmem] * 3,
        out_specs=hbm,
        out_shape=pltpu.HBM((Y, ZH, 64, 128), BF16),
        scratch_shapes=[pltpu.SemaphoreType.DMA((Y, 3))],
        cost_estimate=pl.CostEstimate(flops=4000000000, transcendentals=0, bytes_accessed=1 << 18),
        compiler_params=SMALL,
        name="fan",
    )(*on_chip(row, first, other))
    sends, cols = lax.optimization_barrier((sends, cols))
    over_y = lax.all_to_all(sends, "y", 0, 0, tiled=True, axis_index_groups=[Y_ORDER])
    everything = lax.all_gather(over_y, "core", axis=0, tiled=False)
    q, uu = pl.pallas_call(
        left_kernel,
        in_specs=[vmem] * 3,
        out_specs=(vmem, vmem),
        out_shape=(pltpu.VMEM((2 * R, B), BF16), pltpu.VMEM((B, 2 * R), BF16)),
        compiler_params=SMALL,
        name="left",
    )(*on_chip(cols), *off_chip(diag_upper_inv, diag_lower_inv))
    return pl.pallas_call(
        schur_kernel,
        in_specs=[pl.BlockSpec(memory_space=pltpu.SMEM)] + [vmem] * 7,
        out_specs=hbm,
        out_shape=jax.ShapeDtypeStruct((B, 4 * B), BF16),
        scratch_shapes=[
            pltpu.VMEM((4, B, B), BF16),
            pltpu.SemaphoreType.DMA((4, 4)),
        ],
        name="schur",
    )(lax.axis_index("zh")[None], *on_chip(everything.reshape(CORE, Y, ZH, 64, 128), q, uu, *held))


def solution(mesh):
    parts = Mesh(mesh.devices.reshape(Y, ZH, CORE, C), ROW + COL)
    placed = (
        P(ROW, COL),
        P(ROW, COL, None),
        P(ROW, COL, None),
        P(COL, ROW, None),
        P(COL, ROW, None),
        P(),
        P(),
    )
    return jax.shard_map(
        shards, mesh=parts, in_specs=placed, out_specs=P(ROW, COL), check_vma=False
    )
```
